128 devices in a mesh: region: 8 (over y, core), slab: 16 (over x, z).
Axes of the slice: x: 4, y: 4, z: 4, core: 2. Of those that a mesh axis runs over, the one named last changes fastest.
Arguments:
- coarse: float32 [32, 176, 8, 256], P('region', 'slab'), may hold values from -6 to 6
- cover: int32 [8, 16, 16, 3], replicated, may hold values from 0 to 175, as said below
- sizes: int32 [8, 2], replicated, may hold values from 6 to 16, as said below
- tclass: int32 [8, 48, 192], P('region'), may hold values from 0 to 15
- up_rows: float32 [384, 128], replicated, may hold values from -0.5 to 0.5
- up_cols: float32 [128, 1536], replicated, may hold values from -0.5 to 0.5
- lift: float32 [32, 64], replicated, may hold values from -1 to 1
- kernel_one: bfloat16 [3, 3, 64, 64], replicated, may hold values from -0.25 to 0.25
- kernel_two: bfloat16 [3, 3, 64, 64], replicated, may hold values from -0.25 to 0.25
- gain_table: float32 [16, 64], replicated, may hold values from 0.1 to 1.9
- shift_table: float32 [16, 64], replicated, may hold values from -3 to 3
Outputs:
- fine_out: bfloat16 [8, 384, 98304], P('region', 'slab')
The draws below stay inside these ranges and needn't reach their ends.
Inputs may be any that keep to these rules, and one draw needn't show every extreme that they name: `cover`: for each region r there is an anchor (g, h) such that entry (r, i, j) names global block row g + i and block column (h + j) % 176 (longitude wraps around), as owner (g + i) // 4, row (g + i) % 4 and that column. `sizes`: column 0 lies in 6 to 16, column 1 in 6 to 16; in every draw one region has both full and another has both least.
All inputs are finite; a program needn't handle non-finite values.
Results may differ from the reference program's by a relative error of at most 0.0053.
Values may be sent and summed in bfloat16 or wider, within the bound.
A program may use at most 192 MiB of HBM per device.

```python
import jax
import jax.numpy as jnp
from jax import lax

CIN = 32
CH = 64
CLASSES = 16
BH = 8
BW = 8
KR = 16
KC = 16
BROW_OWN = 4
FW = 1536
TILE = 8
REGIONS = 8
BROWS = 32
BCOLS = 176
FH = 384
PH = 128
PW = 128


def draw_cover(key, part):
    key_rows, key_cols, key_pick = jax.random.split(key, 3)
    row_start = jax.random.randint(key_rows, (REGIONS,), 0, BROWS - KR + 1)
    col_start = jax.random.randint(key_cols, (REGIONS,), 0, BCOLS)
    chosen = jax.random.randint(key_pick, (), 0, REGIONS)
    region_ids = jnp.arange(REGIONS, dtype=jnp.int32)
    row_start = jnp.where(region_ids == chosen, 0, row_start)
    col_start = jnp.where(region_ids == chosen, BCOLS - KC, col_start)
    global_rows = row_start[:, None, None] + jnp.arange(KR, dtype=jnp.int32)[None, :, None] + jnp.zeros((1, 1, KC), jnp.int32)
    global_cols = (col_start[:, None, None] + jnp.arange(KC, dtype=jnp.int32)[None, None, :] + jnp.zeros((1, KR, 1), jnp.int32)) % BCOLS
    return jnp.stack([global_rows // BROW_OWN, global_rows % BROW_OWN, global_cols], axis=-1).astype(jnp.int32)


def draw_sizes(key, part):
    key_rows, key_cols, key_pick = jax.random.split(key, 3)
    low_rows = (KR + 2) // 3
    low_cols = (KC + 2) // 3
    extent_rows = jax.random.randint(key_rows, (REGIONS,), low_rows, KR + 1)
    extent_cols = jax.random.randint(key_cols, (REGIONS,), low_cols, KC + 1)
    chosen = jax.random.randint(key_pick, (), 0, REGIONS)
    region_ids = jnp.arange(REGIONS, dtype=jnp.int32)
    full_one = region_ids == chosen
    least_one = region_ids == (chosen + 1) % REGIONS
    extent_rows = jnp.where(full_one, KR, jnp.where(least_one, low_rows, extent_rows))
    extent_cols = jnp.where(full_one, KC, jnp.where(least_one, low_cols, extent_cols))
    return jnp.stack([extent_rows, extent_cols], axis=-1).astype(jnp.int32)


def touch_ends(drawn, key, smallest, largest):
    shape = drawn.shape
    spot = [jax.random.randint(jax.random.fold_in(key, axis), (), 0, shape[axis]) for axis in range(len(shape))]
    drawn = drawn.at[tuple(spot)].set(smallest)
    longest = shape.index(max(shape))
    spot[longest] = (spot[longest] + 1) % shape[longest]
    return drawn.at[tuple(spot)].set(largest)


def steps_of(own_key, dims, cuts, smallest, high):
    loudness = 1.0
    for dim, parts in cuts:
        draws = jax.random.uniform(jax.random.fold_in(jax.random.fold_in(own_key, 6), dim), (parts,), jnp.float32, smallest / len(cuts), high / len(cuts))
        loudness = loudness * jnp.repeat(jnp.exp(draws), dims[dim] // parts).reshape((-1,) + (1,) * (len(dims) - 1 - dim))
    return loudness


def centred(own_key, extent, scale, bound, cuts=(), kind=jnp.bfloat16):
    drawn = jax.random.normal(own_key, extent, jnp.float32) * scale
    if len(cuts) > 0:
        drawn = steps_of(own_key, extent, cuts, -0.22, 0.18) * drawn
    return jnp.clip(drawn, min=-bound, max=bound).astype(kind)


def setup_inputs(seed: int = 0) -> dict:
    key_of = jax.random.split(jax.random.key(seed), 12)
    return {
        "coarse": centred(key_of[0], (BROWS, BCOLS, BH, BW * CIN), 1.0, 6.0, ((0, 8), (1, 16)), jnp.float32),
        "cover": draw_cover(jax.random.fold_in(key_of[11], 71), 0),
        "sizes": draw_sizes(jax.random.fold_in(key_of[11], 71), 0),
        "tclass": touch_ends(jax.random.randint(key_of[3], (REGIONS, FH // TILE, FW // TILE), 0, CLASSES), jax.random.fold_in(key_of[3], 1), 0, CLASSES - 1).astype(jnp.int32),
        "up_rows": centred(key_of[4], (FH, PH), PH ** -0.5, 0.5, (), jnp.float32),
        "up_cols": centred(key_of[5], (PW, FW), PW ** -0.5, 0.5, (), jnp.float32),
        "lift": centred(key_of[6], (CIN, CH), CIN ** -0.5, 1.0, (), jnp.float32),
        "kernel_one": centred(key_of[7], (3, 3, CH, CH), (9 * CH) ** -0.5, 0.25),
        "kernel_two": centred(key_of[8], (3, 3, CH, CH), (9 * CH) ** -0.5, 0.25),
        "gain_table": jnp.clip(1.0 + 0.18 * jax.random.normal(key_of[9], (CLASSES, CH), jnp.float32), 0.1, 1.9),
        "shift_table": centred(key_of[10], (CLASSES, CH), 0.5, 3.0, (), jnp.float32),
    }


def conv_same(field, kernel):
    widened = field[None].astype(jnp.float32)
    output = lax.conv_general_dilated(widened, kernel.astype(jnp.float32), (1, 1), 'SAME', dimension_numbers=('NHWC', 'HWIO', 'NHWC'), precision=lax.Precision.HIGHEST)
    return output[0]


def reference(coarse, cover, sizes, tclass, up_rows, up_cols, lift, kernel_one, kernel_two, gain_table, shift_table):
    def one_region(index):
        covered = cover[index]
        global_rows = covered[..., 0] * BROW_OWN + covered[..., 1]
        blocks = coarse[global_rows, covered[..., 2]]
        patch = jnp.transpose(blocks, (0, 2, 1, 3)).reshape(PH, PW * CIN)
        rows_up = jnp.dot(up_rows, patch, precision=lax.Precision.HIGHEST, preferred_element_type=jnp.float32).reshape(FH, PW, CIN)
        upsampled = jnp.einsum('ybc,bx->yxc', rows_up, up_cols, precision=lax.Precision.HIGHEST)
        lifted = jnp.einsum('yxc,cd->yxd', upsampled, lift, precision=lax.Precision.HIGHEST)
        size_row = sizes[index]
        valid_rows = size_row[0] * (FH // KR)
        valid_cols = size_row[1] * (FW // KC)
        inside = (jnp.arange(FH, dtype=jnp.int32)[:, None] < valid_rows) & (jnp.arange(FW, dtype=jnp.int32)[None, :] < valid_cols)
        fine_in = jnp.where(inside[..., None], lifted, 0.0).astype(jnp.bfloat16)
        activated = jax.nn.silu(fine_in.astype(jnp.float32)).astype(jnp.bfloat16)
        first_conv = conv_same(activated, kernel_one)
        classes = jnp.repeat(jnp.repeat(tclass[index], TILE, axis=0), TILE, axis=1)
        modulated = first_conv * gain_table[classes] + shift_table[classes]
        hidden = jnp.where(inside[..., None], jax.nn.silu(modulated), 0.0).astype(jnp.bfloat16)
        second_conv = conv_same(hidden, kernel_two)
        result = jnp.where(inside[..., None], fine_in.astype(jnp.float32) + second_conv, 0.0)
        return result.astype(jnp.bfloat16).reshape(FH, FW * CH)

    return lax.map(one_region, jnp.arange(REGIONS, dtype=jnp.int32))
```

```python
import jax
import jax.numpy as jnp
from jax import lax
from jax.experimental import pallas as pl
from jax.experimental.pallas import tpu as pltpu
from jax.sharding import PartitionSpec as P

BF = jnp.bfloat16
F32 = jnp.float32
ROWS = 24
HALO = 32
PAIRS = 768


def split_hi_lo(value):
    hi = value.astype(BF)
    lo = (value - hi.astype(F32)).astype(BF)
    return hi, lo


def silu(value):
    half = 0.5 * value
    return half + half * jnp.tanh(half)


def build_conv_weights(kernel_ref, out_ref):
    empty = jnp.zeros((64, 64), F32)
    for row_in in range(4):
        for slot, pixel in enumerate((0, 1, 2, -1)):
            for row_out in range(2):
                parts = []
                for pixel_out in range(2):
                    p = row_in - row_out
                    q = pixel - pixel_out + 1
                    if 0 <= p <= 2 and 0 <= q <= 2:
                        parts.append(kernel_ref[p, q].astype(F32))
                    else:
                        parts.append(empty)
                out_ref[pl.ds(row_in * 256 + slot * 64, 64), pl.ds(row_out * 128, 128)] = jnp.concatenate(
                    parts, axis=1
                ).astype(BF)


def compute_kernel(
    sc_ref,
    rows_ref,
    lift_ref,
    uc_ref,
    k1_ref,
    k2_ref,
    onehot_ref,
    table_ref,
    out_ref,
    w1,
    w2,
    lifted,
    act_in,
    hid_in,
    fine,
    maps,
    shifted,
    result,
):
    start = sc_ref[0]
    valid_rows = sc_ref[1]
    valid_pairs = sc_ref[2]
    first_row = sc_ref[3]

    build_conv_weights(k1_ref, w1)
    build_conv_weights(k2_ref, w2)
    for tile_row in range(5):
        maps[tile_row] = jnp.dot(onehot_ref[tile_row], table_ref[...], preferred_element_type=F32)
    for place in range(16):
        slot = lax.rem(place + start, 16)
        block = rows_ref[slot]
        block = jnp.concatenate([block, block], axis=1)
        value = jnp.dot(block, lift_ref[...], preferred_element_type=F32)
        for w in range(4):
            lifted[pl.ds((w * 16 + place) * HALO, HALO), :] = value[:, w * 128 : (w + 1) * 128]

    zeros8 = jnp.zeros((8, 128), F32)
    for row in range(2):
        shifted[row, pl.ds(0, 8), :] = zeros8
        shifted[row, pl.ds(8 + PAIRS, 8), :] = zeros8
    pair_ids = lax.broadcasted_iota(jnp.int32, (PAIRS, 128), 0)
    lane_low = lax.broadcasted_iota(jnp.int32, (PAIRS, 128), 1) < 64
    col_valid = pair_ids < valid_pairs
    low16 = lax.broadcasted_iota(jnp.int32, (16, 128), 1) < 64

    def spread(row, value, dst_ref, pair):
        shifted[row, pl.ds(8, PAIRS), :] = value
        after = shifted[row, pl.ds(9, PAIRS), :]
        before = shifted[row, pl.ds(7, PAIRS), :]
        dst_ref[pair, :, pl.ds(row * 256, 128)] = value.astype(BF)
        dst_ref[pair, :, pl.ds(row * 256 + 128, 128)] = jnp.where(lane_low, after, before).astype(BF)

    def stage_one(pair, carry):
        sides = []
        for row in range(2):
            parts = []
            for w in range(4):
                got = lifted[pl.ds(w * 16 * HALO + pair * 2 + row, 16, stride=HALO), :]
                turned = pltpu.roll(got, 64, 1)
                parts += [
                    jnp.where(low16, got, 0.0),
                    jnp.where(low16, 0.0, got),
                    jnp.where(low16, turned, 0.0),
                    jnp.where(low16, 0.0, turned),
                ]
            side = jnp.concatenate(parts, axis=0).astype(BF)
            sides.append(jnp.concatenate([side, side], axis=0))
        value = jnp.dot(uc_ref[...], jnp.concatenate(sides, axis=1), preferred_element_type=F32)
        for row in range(2):
            global_row = first_row + pair * 2 + row
            keep = col_valid & ((global_row >= 0) & (global_row < valid_rows))
            rounded = jnp.where(keep, value[:, row * 128 : (row + 1) * 128], 0.0).astype(BF)
            fine[pair, :, pl.ds(row * 128, 128)] = rounded
            spread(row, silu(rounded.astype(F32)), act_in, pair)
        return carry

    lax.fori_loop(0, 14, stage_one, 0)

    def conv(src_ref, pair, w_ref):
        window = jnp.concatenate([src_ref[pair], src_ref[pair + 1]], axis=1)
        return jnp.dot(window, w_ref[...], preferred_element_type=F32)

    def stage_two(pair, carry):
        value = conv(act_in, pair, w1)
        for row in range(2):
            local_row = pair * 2 + row
            tile_row = lax.div(local_row + 7, 8)
            global_row = first_row + 1 + local_row
            gain = maps[tile_row, :, pl.ds(0, 128)]
            shift = maps[tile_row, :, pl.ds(128, 128)]
            keep = col_valid & ((global_row >= 0) & (global_row < valid_rows))
            moved = value[:, row * 128 : (row + 1) * 128] * gain + shift
            spread(row, jnp.where(keep, silu(moved), 0.0), hid_in, pair)
        return carry

    lax.fori_loop(0, 13, stage_two, 0)

    def stage_three(pair, carry):
        value = conv(hid_in, pair, w2)
        for row in range(2):
            global_row = first_row + 2 + pair * 2 + row
            keep = col_valid & (global_row < valid_rows)
            total = fine[pair + 1, :, pl.ds(row * 128, 128)].astype(F32) + value[:, row * 128 : (row + 1) * 128]
            at = pl.multiple_of((pair * 2 + row) * PAIRS, PAIRS)
            result[pl.ds(at, PAIRS), :] = jnp.where(keep, total, 0.0)
        return carry

    lax.fori_loop(0, 12, stage_three, 0)

    def emit(group, carry):
        for k in range(16):
            p = group * 16 + k
            got = [result[pl.ds(p + 8 * r * PAIRS, 8, stride=PAIRS), :] for r in range(3)]
            out_ref[:, pl.ds(pl.multiple_of(p * 128, 128), 128)] = jnp.concatenate(got, axis=0).astype(BF)
        return carry

    lax.fori_loop(0, PAIRS // 16, emit, 0)


def compute(scalars, rows, lift_w, uc, kernel_one, kernel_two, onehot, table):
    vmem = pl.BlockSpec(memory_space=pltpu.VMEM)
    return pl.pallas_call(
        compute_kernel,
        out_shape=jax.ShapeDtypeStruct((ROWS, PAIRS * 128), BF),
        in_specs=[pl.BlockSpec(memory_space=pltpu.SMEM)] + [vmem] * 7,
        out_specs=vmem,
        scratch_shapes=[
            pltpu.VMEM((1024, 256), BF),
            pltpu.VMEM((1024, 256), BF),
            pltpu.VMEM((4 * 16 * HALO, 128), F32),
            pltpu.VMEM((14, PAIRS, 512), BF),
            pltpu.VMEM((13, PAIRS, 512), BF),
            pltpu.VMEM((14, PAIRS, 256), BF),
            pltpu.VMEM((5, PAIRS, 256), F32),
            pltpu.VMEM((2, PAIRS + 16, 128), F32),
            pltpu.VMEM((ROWS * PAIRS, 128), F32),
        ],
        compiler_params=pltpu.CompilerParams(vmem_limit_bytes=63 * 1024 * 1024),
        name="block",
    )(scalars, rows, lift_w, uc, kernel_one, kernel_two, onehot, table)


def local(
    coarse,
    cover,
    sizes,
    tclass,
    up_rows,
    up_cols,
    lift,
    kernel_one,
    kernel_two,
    gain_table,
    shift_table,
):
    region = lax.axis_index("region")
    slab = lax.axis_index("slab")
    columns = jnp.transpose(coarse.astype(BF), (1, 0, 2, 3)).reshape(11, 32, 256)
    columns = jnp.concatenate([columns, jnp.zeros((5, 32, 256), BF)], axis=0)
    columns = jnp.concatenate([columns, columns], axis=0)
    columns = lax.dynamic_slice_in_dim(columns, lax.rem(5 * slab, 16), 16, 0)
    columns = lax.all_to_all(columns, "slab", split_axis=0, concat_axis=0, tiled=True)
    starts = cover[:, 0, 0, 2]
    place = jnp.remainder(slab - starts, 16)
    wanted = jnp.remainder(starts + place, 176) // 11
    picked = columns[wanted]
    mine = lax.all_to_all(picked, "region", split_axis=0, concat_axis=0, tiled=True)
    first_block = cover[region, 0, 0, 0] * 4 + cover[region, 0, 0, 1]
    patch = lax.dynamic_slice_in_dim(mine.reshape(256, 256), first_block * 8, 128, 0)
    padded_rows = jnp.pad(up_rows, ((2, 6), (0, 0)))
    rows_w = jnp.concatenate([padded_rows[24 * s : 24 * s + HALO] for s in range(16)], axis=0)
    rows_hi, rows_lo = split_hi_lo(rows_w)
    up = jnp.dot(
        jnp.concatenate([rows_hi, rows_lo], axis=1),
        jnp.concatenate([patch, patch], axis=0),
        preferred_element_type=F32,
    )
    up = up.astype(BF).reshape(16, HALO, 256)
    up = lax.all_to_all(up, "slab", split_axis=0, concat_axis=0, tiled=True)

    cols = up_cols.reshape(16, 4, 2, PAIRS, 2)
    variants = [cols[:, :, q, :, par] for q, par in ((0, 0), (1, 1), (1, 0), (0, 1))]
    uc = jnp.stack(variants, axis=0)
    uc = jnp.transpose(uc, (3, 2, 0, 1)).reshape(PAIRS, 256)
    uc = jnp.concatenate(split_hi_lo(uc), axis=1)
    lift_hi, lift_lo = split_hi_lo(lift)
    eye = jnp.eye(8, dtype=BF)
    lift_w = jnp.concatenate([jnp.kron(eye, lift_hi), jnp.kron(eye, lift_lo)], axis=0)

    tile_rows = 3 * slab - 1 + jnp.arange(5, dtype=jnp.int32)
    classes = tclass[0][jnp.clip(tile_rows, 0, 47)]
    onehot = (classes[..., None] == jnp.arange(32, dtype=jnp.int32) % 16).astype(BF)
    onehot = jnp.broadcast_to(onehot[:, :, None, :], (5, 192, 4, 32)).reshape(5, PAIRS, 32)
    table = jnp.concatenate([gain_table, gain_table, shift_table, shift_table], axis=1)
    table = jnp.concatenate(split_hi_lo(table), axis=0)
    scalars = jnp.stack(
        [
            lax.rem(cover[region, 0, 0, 2], 16),
            sizes[region, 0] * 24,
            sizes[region, 1] * 48,
            slab * 24 - 2,
        ]
    ).astype(jnp.int32)
    out = compute(scalars, up, lift_w, uc, kernel_one, kernel_two, onehot, table)
    return out[None]


def solution(mesh):
    return jax.shard_map(
        local,
        mesh=mesh,
        in_specs=(
            P("region", "slab", None, None),
            P(),
            P(),
            P("region", None, None),
            P(),
            P(),
            P(),
            P(),
            P(),
            P(),
            P(),
        ),
        out_specs=P("region", "slab", None),
        check_vma=False,
    )
```

```python
import jax
import jax.numpy as jnp
from jax import lax
from jax.experimental import pallas as pl
from jax.experimental.pallas import tpu as pltpu
from jax.sharding import PartitionSpec as P

BF = jnp.bfloat16
F32 = jnp.float32
ROWS = 24
HALO = 32
PAIRS = 768


def split_hi_lo(value):
    hi = value.astype(BF)
    lo = (value - hi.astype(F32)).astype(BF)
    return hi, lo


def silu(value):
    half = 0.5 * value
    return half + half * jnp.tanh(half)


def build_conv_weights(kernel_ref, out_ref):
    empty = jnp.zeros((64, 64), F32)
    for row_in in range(4):
        for slot, pixel in enumerate((0, 1, 2, -1)):
            for row_out in range(2):
                parts = []
                for pixel_out in range(2):
                    p = row_in - row_out
                    q = pixel - pixel_out + 1
                    if 0 <= p <= 2 and 0 <= q <= 2:
                        parts.append(kernel_ref[p, q].astype(F32))
                    else:
                        parts.append(empty)
                out_ref[pl.ds(row_in * 256 + slot * 64, 64), pl.ds(row_out * 128, 128)] = jnp.concatenate(
                    parts, axis=1
                ).astype(BF)


def prepare_columns(cols_ref, split, uc):
    source = lax.broadcasted_iota(jnp.int32, (256, 256), 0)
    target = lax.broadcasted_iota(jnp.int32, (256, 256), 1)
    chosen = jnp.where(target < 128, 2 * target, 2 * target - 255)
    select = (source == chosen).astype(F32).astype(BF)
    for chunk in range(6):
        halves = split_hi_lo(cols_ref[:, pl.ds(chunk * 256, 256)])
        for part in range(2):
            value = jnp.dot(halves[part], select, preferred_element_type=F32)
            split[pl.ds(part * 256, 128), :] = value[:, :128]
            split[pl.ds(part * 256 + 128, 128), :] = value[:, 128:]
        for part in range(2):
            pieces = []
            for w in range(4):
                for q, parity in ((0, 0), (1, 1), (1, 0), (0, 1)):
                    pieces.append(split[pl.ds(part * 256 + parity * 128 + 2 * w + q, 16, stride=8), :])
            block = jnp.concatenate(pieces, axis=0).T
            uc[pl.ds(chunk * 128, 128), pl.ds(part * 256, 256)] = block.astype(BF)


def prepare_lift(lift_ref, lift_w):
    empty = jnp.zeros((32, 64), F32)
    lift_w[...] = jnp.zeros_like(lift_w)
    for part, value in enumerate(split_hi_lo(lift_ref[...])):
        value = value.astype(F32)
        sides = (jnp.concatenate([value, empty], axis=1), jnp.concatenate([empty, value], axis=1))
        for bw in range(8):
            lift_w[pl.ds(part * 256 + bw * 32, 32), pl.ds(bw // 2 * 128, 128)] = sides[bw % 2].astype(BF)


def prepare_maps(class_ref, gain_ref, shift_ref, maps):
    gain, shift = gain_ref[...], shift_ref[...]
    table = jnp.concatenate(split_hi_lo(jnp.concatenate([gain, gain, shift, shift], axis=1)), axis=0)
    owner = lax.broadcasted_iota(jnp.int32, (192, PAIRS), 1) // 4
    widen = (owner == lax.broadcasted_iota(jnp.int32, (192, PAIRS), 0)).astype(F32).astype(BF)
    ids = lax.broadcasted_iota(jnp.int32, (32, 192), 0) % 16
    hots = []
    for tile_row in range(5):
        hots.append((class_ref[pl.ds(tile_row, 1), :] == ids).astype(F32))
    wide = jnp.dot(jnp.concatenate(hots, axis=0).astype(BF), widen, preferred_element_type=F32)
    for tile_row in range(5):
        hot = wide[tile_row * 32 : (tile_row + 1) * 32].T.astype(BF)
        maps[tile_row] = jnp.dot(hot, table, preferred_element_type=F32)


def compute_kernel(
    sc_ref,
    rows_ref,
    lift_ref,
    cols_ref,
    k1_ref,
    k2_ref,
    class_ref,
    gain_ref,
    shift_ref,
    out_ref,
    w1,
    w2,
    lift_w,
    split,
    uc,
    lifted,
    act_in,
    hid_in,
    fine,
    maps,
    shifted,
    result,
):
    start = sc_ref[0]
    valid_rows = sc_ref[1]
    valid_pairs = sc_ref[2]
    first_row = sc_ref[3]

    build_conv_weights(k1_ref, w1)
    build_conv_weights(k2_ref, w2)
    prepare_columns(cols_ref, split, uc)
    prepare_lift(lift_ref, lift_w)
    prepare_maps(class_ref, gain_ref, shift_ref, maps)
    for place in range(16):
        slot = lax.rem(place + start, 16)
        block = rows_ref[slot]
        block = jnp.concatenate([block, block], axis=1)
        value = jnp.dot(block, lift_w[...], preferred_element_type=F32)
        for w in range(4):
            lifted[pl.ds((w * 16 + place) * HALO, HALO), :] = value[:, w * 128 : (w + 1) * 128]

    zeros8 = jnp.zeros((8, 128), F32)
    for row in range(2):
        shifted[row, pl.ds(0, 8), :] = zeros8
        shifted[row, pl.ds(8 + PAIRS, 8), :] = zeros8
    pair_ids = lax.broadcasted_iota(jnp.int32, (PAIRS, 128), 0)
    lane_low = lax.broadcasted_iota(jnp.int32, (PAIRS, 128), 1) < 64
    col_valid = pair_ids < valid_pairs
    low16 = lax.broadcasted_iota(jnp.int32, (16, 128), 1) < 64

    def spread(row, value, dst_ref, pair):
        shifted[row, pl.ds(8, PAIRS), :] = value
        after = shifted[row, pl.ds(9, PAIRS), :]
        before = shifted[row, pl.ds(7, PAIRS), :]
        dst_ref[pair, :, pl.ds(row * 256, 128)] = value.astype(BF)
        dst_ref[pair, :, pl.ds(row * 256 + 128, 128)] = jnp.where(lane_low, after, before).astype(BF)

    def stage_one(pair, carry):
        sides = []
        for row in range(2):
            parts = []
            for w in range(4):
                got = lifted[pl.ds(w * 16 * HALO + pair * 2 + row, 16, stride=HALO), :]
                turned = pltpu.roll(got, 64, 1)
                parts += [
                    jnp.where(low16, got, 0.0),
                    jnp.where(low16, 0.0, got),
                    jnp.where(low16, turned, 0.0),
                    jnp.where(low16, 0.0, turned),
                ]
            side = jnp.concatenate(parts, axis=0).astype(BF)
            sides.append(jnp.concatenate([side, side], axis=0))
        value = jnp.dot(uc[...], jnp.concatenate(sides, axis=1), preferred_element_type=F32)
        for row in range(2):
            global_row = first_row + pair * 2 + row
            keep = col_valid & ((global_row >= 0) & (global_row < valid_rows))
            rounded = jnp.where(keep, value[:, row * 128 : (row + 1) * 128], 0.0).astype(BF)
            fine[pair, :, pl.ds(row * 128, 128)] = rounded
            spread(row, silu(rounded.astype(F32)), act_in, pair)
        return carry

    lax.fori_loop(0, 14, stage_one, 0)

    def conv(src_ref, pair, w_ref):
        window = jnp.concatenate([src_ref[pair], src_ref[pair + 1]], axis=1)
        return jnp.dot(window, w_ref[...], preferred_element_type=F32)

    def stage_two(pair, carry):
        value = conv(act_in, pair, w1)
        for row in range(2):
            local_row = pair * 2 + row
            tile_row = lax.div(local_row + 7, 8)
            global_row = first_row + 1 + local_row
            gain = maps[tile_row, :, pl.ds(0, 128)]
            shift = maps[tile_row, :, pl.ds(128, 128)]
            keep = col_valid & ((global_row >= 0) & (global_row < valid_rows))
            moved = value[:, row * 128 : (row + 1) * 128] * gain + shift
            spread(row, jnp.where(keep, silu(moved), 0.0), hid_in, pair)
        return carry

    lax.fori_loop(0, 13, stage_two, 0)

    def stage_three(pair, carry):
        value = conv(hid_in, pair, w2)
        for row in range(2):
            global_row = first_row + 2 + pair * 2 + row
            keep = col_valid & (global_row < valid_rows)
            total = fine[pair + 1, :, pl.ds(row * 128, 128)].astype(F32) + value[:, row * 128 : (row + 1) * 128]
            at = pl.multiple_of((pair * 2 + row) * PAIRS, PAIRS)
            result[pl.ds(at, PAIRS), :] = jnp.where(keep, total, 0.0)
        return carry

    lax.fori_loop(0, 12, stage_three, 0)

    def emit(group, carry):
        for k in range(16):
            p = group * 16 + k
            got = [result[pl.ds(p + 8 * r * PAIRS, 8, stride=PAIRS), :] for r in range(3)]
            out_ref[:, pl.ds(pl.multiple_of(p * 128, 128), 128)] = jnp.concatenate(got, axis=0).astype(BF)
        return carry

    lax.fori_loop(0, PAIRS // 16, emit, 0)


def compute(scalars, *operands):
    vmem = pl.BlockSpec(memory_space=pltpu.VMEM)
    return pl.pallas_call(
        compute_kernel,
        out_shape=jax.ShapeDtypeStruct((ROWS, PAIRS * 128), BF),
        in_specs=[pl.BlockSpec(memory_space=pltpu.SMEM)] + [vmem] * len(operands),
        out_specs=vmem,
        scratch_shapes=[
            pltpu.VMEM((1024, 256), BF),
            pltpu.VMEM((1024, 256), BF),
            pltpu.VMEM((512, 512), BF),
            pltpu.VMEM((512, 128), F32),
            pltpu.VMEM((PAIRS, 512), BF),
            pltpu.VMEM((4 * 16 * HALO, 128), F32),
            pltpu.VMEM((14, PAIRS, 512), BF),
            pltpu.VMEM((13, PAIRS, 512), BF),
            pltpu.VMEM((14, PAIRS, 256), BF),
            pltpu.VMEM((5, PAIRS, 256), F32),
            pltpu.VMEM((2, PAIRS + 16, 128), F32),
            pltpu.VMEM((ROWS * PAIRS, 128), F32),
        ],
        compiler_params=pltpu.CompilerParams(vmem_limit_bytes=63 * 1024 * 1024),
        name="block",
    )(scalars, *operands)


def local(
    coarse,
    cover,
    sizes,
    tclass,
    up_rows,
    up_cols,
    lift,
    kernel_one,
    kernel_two,
    gain_table,
    shift_table,
):
    region = lax.axis_index("region")
    slab = lax.axis_index("slab")
    columns = jnp.transpose(coarse.astype(BF), (1, 0, 2, 3)).reshape(11, 32, 256)
    columns = jnp.concatenate([columns, jnp.zeros((5, 32, 256), BF)], axis=0)
    columns = jnp.concatenate([columns, columns], axis=0)
    columns = lax.dynamic_slice_in_dim(columns, lax.rem(5 * slab, 16), 16, 0)
    columns = lax.all_to_all(columns, "slab", split_axis=0, concat_axis=0, tiled=True)
    starts = cover[:, 0, 0, 2]
    place = jnp.remainder(slab - starts, 16)
    wanted = jnp.remainder(starts + place, 176) // 11
    picked = columns[wanted]
    mine = lax.all_to_all(picked, "region", split_axis=0, concat_axis=0, tiled=True)
    first_block = cover[region, 0, 0, 0] * 4 + cover[region, 0, 0, 1]
    patch = lax.dynamic_slice_in_dim(mine.reshape(256, 256), first_block * 8, 128, 0)
    padded_rows = jnp.pad(up_rows, ((2, 6), (0, 0)))
    rows_w = jnp.concatenate([padded_rows[24 * s : 24 * s + HALO] for s in range(16)], axis=0)
    rows_hi = lax.reduce_precision(rows_w, 8, 7)
    rows_w = jnp.concatenate([rows_hi.astype(BF), (rows_w - rows_hi).astype(BF)], axis=1)
    up = jnp.dot(rows_w, jnp.concatenate([patch, patch], axis=0), preferred_element_type=F32)
    up = up.astype(BF).reshape(16, HALO, 256)
    up = lax.all_to_all(up, "slab", split_axis=0, concat_axis=0, tiled=True)

    tile_rows = jnp.clip(3 * slab - 1 + jnp.arange(8, dtype=jnp.int32), 0, 47)
    classes = tclass[0][tile_rows]
    scalars = jnp.stack(
        [
            lax.rem(cover[region, 0, 0, 2], 16),
            sizes[region, 0] * 24,
            sizes[region, 1] * 48,
            slab * 24 - 2,
        ]
    ).astype(jnp.int32)
    out = compute(scalars, up, lift, up_cols, kernel_one, kernel_two, classes, gain_table, shift_table)
    return out[None]


def solution(mesh):
    return jax.shard_map(
        local,
        mesh=mesh,
        in_specs=(
            P("region", "slab", None, None),
            P(),
            P(),
            P("region", None, None),
            P(),
            P(),
            P(),
            P(),
            P(),
            P(),
            P(),
        ),
        out_specs=P("region", "slab", None),
        check_vma=False,
    )
```

```python
import jax
import jax.numpy as jnp
from jax import lax
from jax.experimental import pallas as pl
from jax.experimental.pallas import tpu as pltpu
from jax.sharding import PartitionSpec as P

BF = jnp.bfloat16
F32 = jnp.float32
ROWS = 24
HALO = 32
PAIRS = 768


def split_hi_lo(value):
    hi = value.astype(BF)
    lo = (value - hi.astype(F32)).astype(BF)
    return hi, lo


def silu(value):
    half = 0.5 * value
    return half + half * jnp.tanh(half)


def build_conv_weights(kernel_ref, out_ref):
    empty = jnp.zeros((64, 64), F32)
    for row_in in range(4):
        for slot, pixel in enumerate((0, 1, 2, -1)):
            for row_out in range(2):
                parts = []
                for pixel_out in range(2):
                    p = row_in - row_out
                    q = pixel - pixel_out + 1
                    if 0 <= p <= 2 and 0 <= q <= 2:
                        parts.append(kernel_ref[p, q].astype(F32))
                    else:
                        parts.append(empty)
                out_ref[pl.ds(row_in * 256 + slot * 64, 64), pl.ds(row_out * 128, 128)] = jnp.concatenate(
                    parts, axis=1
                ).astype(BF)


MESH = pl.DeviceIdType.MESH


def exchange_kernel(
    heads_ref,
    coarse_ref,
    up_ref,
    out_ref,
    cols_send,
    cols_recv,
    pick_send,
    pick_recv,
    rows_send,
    rows_recv,
    padded,
    weights,
    send_one,
    recv_one,
    send_two,
    recv_two,
    send_three,
    recv_three,
):
    region = lax.axis_index("region")
    slab = lax.axis_index("slab")

    barrier = pltpu.get_barrier_semaphore()

    def greet_slab(step, carry):
        pl.semaphore_signal(barrier, inc=1, device_id={"slab": lax.rem(slab + step, 16)}, device_id_type=MESH)
        return carry

    def greet_region(step, carry):
        pl.semaphore_signal(barrier, inc=1, device_id={"region": lax.rem(region + step, 8)}, device_id_type=MESH)
        return carry

    lax.fori_loop(1, 16, greet_slab, 0)
    lax.fori_loop(1, 8, greet_region, 0)
    for t in range(11):
        column = jnp.concatenate([coarse_ref[k, t] for k in range(4)], axis=0)
        cols_send[t] = column.astype(BF)
    pl.semaphore_wait(barrier, 22)

    def copy_one(t, source, target):
        return pltpu.make_async_remote_copy(
            src_ref=cols_send.at[t],
            dst_ref=cols_recv.at[source],
            send_sem=send_one.at[t],
            recv_sem=recv_one.at[source],
            device_id={"slab": target},
            device_id_type=MESH,
        )

    def start_one(t, carry):
        target = lax.rem(11 * slab + t, 16)

        @pl.when(target != slab)
        def _():
            copy_one(t, slab, target).start()

        @pl.when(target == slab)
        def _():
            cols_recv[slab] = cols_send[t]

        return carry

    lax.fori_loop(0, 11, start_one, 0)

    padded[pl.ds(0, 8), :] = jnp.zeros((8, 128), F32)
    padded[pl.ds(8, 384), :] = up_ref[...]
    padded[pl.ds(392, 8), :] = jnp.zeros((8, 128), F32)
    for s in range(16):
        hi, lo = split_hi_lo(padded[pl.ds(24 * s + 6, HALO), :])
        weights[pl.ds(s * HALO, HALO), pl.ds(0, 128)] = hi
        weights[pl.ds(s * HALO, HALO), pl.ds(128, 128)] = lo

    def wait_one(source, carry):
        t = lax.rem(slab + 5 * source, 16)

        @pl.when((t < 11) & (source != slab))
        def _():
            copy_one(0, source, slab).wait_recv()

        return carry

    lax.fori_loop(0, 16, wait_one, 0)

    def copy_two(target, source):
        return pltpu.make_async_remote_copy(
            src_ref=pick_send.at[target],
            dst_ref=pick_recv.at[source],
            send_sem=send_two.at[target],
            recv_sem=recv_two.at[source],
            device_id={"region": target},
            device_id_type=MESH,
        )

    for r in range(8):
        head = heads_ref[3 * r + 2]
        place = lax.rem(slab - head + 176, 16)
        wanted = lax.div(lax.rem(head + place, 176), 11)
        pick_send[r] = cols_recv[wanted]

        @pl.when(region != r)
        def _():
            copy_two(r, region).start()

    pick_recv[region] = pick_send[region]

    def wait_two(step, carry):
        copy_two(0, lax.rem(region + step, 8)).wait_recv()
        return carry

    lax.fori_loop(1, 8, wait_two, 0)

    first = heads_ref[3 * region] * 32 + heads_ref[3 * region + 1] * 8
    row = lax.broadcasted_iota(jnp.int32, (128, 256), 0)
    choose = (row + first == lax.broadcasted_iota(jnp.int32, (128, 256), 1)).astype(F32).astype(BF)
    gathered = jnp.concatenate([pick_recv[b] for b in range(8)], axis=0)
    patch = jnp.dot(choose, gathered, preferred_element_type=F32).astype(BF)
    patch = jnp.concatenate([patch, patch], axis=0)

    def copy_three(target, source):
        return pltpu.make_async_remote_copy(
            src_ref=rows_send.at[target],
            dst_ref=rows_recv.at[source],
            send_sem=send_three.at[target],
            recv_sem=recv_three.at[source],
            device_id={"slab": target},
            device_id_type=MESH,
        )

    for part in range(4):
        value = jnp.dot(weights[pl.ds(part * 128, 128), :], patch, preferred_element_type=F32)
        for k in range(4):
            s = part * 4 + k
            rows_send[s] = value[k * HALO : (k + 1) * HALO].astype(BF)

            @pl.when(slab != s)
            def _():
                copy_three(s, slab).start()

    rows_recv[slab] = rows_send[slab]

    def wait_three(step, carry):
        copy_three(0, lax.rem(slab + step, 16)).wait_recv()
        return carry

    lax.fori_loop(1, 16, wait_three, 0)
    out_ref[...] = rows_recv[...]

    def done_one(t, carry):
        @pl.when(lax.rem(11 * slab + t, 16) != slab)
        def _():
            copy_one(t, slab, slab).wait_send()

        return carry

    lax.fori_loop(0, 11, done_one, 0)

    def done_two(step, carry):
        copy_two(lax.rem(region + step, 8), region).wait_send()
        return carry

    lax.fori_loop(1, 8, done_two, 0)

    def done_three(step, carry):
        copy_three(lax.rem(slab + step, 16), slab).wait_send()
        return carry

    lax.fori_loop(1, 16, done_three, 0)


def exchange(heads, coarse, up_rows):
    vmem = pl.BlockSpec(memory_space=pltpu.VMEM)
    return pl.pallas_call(
        exchange_kernel,
        out_shape=jax.ShapeDtypeStruct((16, HALO, 256), BF),
        in_specs=[pl.BlockSpec(memory_space=pltpu.SMEM), vmem, vmem],
        out_specs=vmem,
        scratch_shapes=[
            pltpu.VMEM((11, 32, 256), BF),
            pltpu.VMEM((16, 32, 256), BF),
            pltpu.VMEM((8, 32, 256), BF),
            pltpu.VMEM((8, 32, 256), BF),
            pltpu.VMEM((16, HALO, 256), BF),
            pltpu.VMEM((16, HALO, 256), BF),
            pltpu.VMEM((400, 128), F32),
            pltpu.VMEM((512, 256), BF),
            pltpu.SemaphoreType.DMA((11,)),
            pltpu.SemaphoreType.DMA((16,)),
            pltpu.SemaphoreType.DMA((8,)),
            pltpu.SemaphoreType.DMA((8,)),
            pltpu.SemaphoreType.DMA((16,)),
            pltpu.SemaphoreType.DMA((16,)),
        ],
        compiler_params=pltpu.CompilerParams(collective_id=0, has_side_effects=True),
        name="exchange",
    )(heads, coarse, up_rows)


def prepare_columns(cols_ref, split, uc):
    source = lax.broadcasted_iota(jnp.int32, (256, 256), 0)
    target = lax.broadcasted_iota(jnp.int32, (256, 256), 1)
    chosen = jnp.where(target < 128, 2 * target, 2 * target - 255)
    select = (source == chosen).astype(F32).astype(BF)
    for chunk in range(6):
        halves = split_hi_lo(cols_ref[:, pl.ds(chunk * 256, 256)])
        for part in range(2):
            value = jnp.dot(halves[part], select, preferred_element_type=F32)
            split[pl.ds(part * 256, 128), :] = value[:, :128]
            split[pl.ds(part * 256 + 128, 128), :] = value[:, 128:]
        for part in range(2):
            pieces = []
            for w in range(4):
                for q, parity in ((0, 0), (1, 1), (1, 0), (0, 1)):
                    pieces.append(split[pl.ds(part * 256 + parity * 128 + 2 * w + q, 16, stride=8), :])
            block = jnp.concatenate(pieces, axis=0).T
            uc[pl.ds(chunk * 128, 128), pl.ds(part * 256, 256)] = block.astype(BF)


def prepare_lift(lift_ref, lift_w):
    empty = jnp.zeros((32, 64), F32)
    lift_w[...] = jnp.zeros_like(lift_w)
    for part, value in enumerate(split_hi_lo(lift_ref[...])):
        value = value.astype(F32)
        sides = (jnp.concatenate([value, empty], axis=1), jnp.concatenate([empty, value], axis=1))
        for bw in range(8):
            lift_w[pl.ds(part * 256 + bw * 32, 32), pl.ds(bw // 2 * 128, 128)] = sides[bw % 2].astype(BF)


def prepare_maps(class_ref, gain_ref, shift_ref, maps):
    gain, shift = gain_ref[...], shift_ref[...]
    table = jnp.concatenate(split_hi_lo(jnp.concatenate([gain, gain, shift, shift], axis=1)), axis=0)
    owner = lax.broadcasted_iota(jnp.int32, (192, PAIRS), 1) // 4
    widen = (owner == lax.broadcasted_iota(jnp.int32, (192, PAIRS), 0)).astype(F32).astype(BF)
    ids = lax.broadcasted_iota(jnp.int32, (32, 192), 0) % 16
    hots = []
    for tile_row in range(5):
        hots.append((class_ref[pl.ds(tile_row, 1), :] == ids).astype(F32))
    wide = jnp.dot(jnp.concatenate(hots, axis=0).astype(BF), widen, preferred_element_type=F32)
    for tile_row in range(5):
        hot = wide[tile_row * 32 : (tile_row + 1) * 32].T.astype(BF)
        maps[tile_row] = jnp.dot(hot, table, preferred_element_type=F32)


def compute_kernel(
    sc_ref,
    rows_ref,
    lift_ref,
    cols_ref,
    k1_ref,
    k2_ref,
    class_ref,
    gain_ref,
    shift_ref,
    out_ref,
    w1,
    w2,
    lift_w,
    split,
    uc,
    lifted,
    act_in,
    hid_in,
    fine,
    maps,
    shifted,
    result,
):
    region = lax.axis_index("region")
    valid_rows = sc_ref[24 + 2 * region] * 24
    valid_pairs = sc_ref[25 + 2 * region] * 48
    first_row = lax.axis_index("slab") * 24 - 2

    build_conv_weights(k1_ref, w1)
    build_conv_weights(k2_ref, w2)
    prepare_columns(cols_ref, split, uc)
    prepare_lift(lift_ref, lift_w)
    prepare_maps(class_ref, gain_ref, shift_ref, maps)
    start = sc_ref[3 * region + 2]
    for place in range(16):
        block = rows_ref[lax.rem(place + start, 16)]
        block = jnp.concatenate([block, block], axis=1)
        value = jnp.dot(block, lift_w[...], preferred_element_type=F32)
        for w in range(4):
            lifted[pl.ds((w * 16 + place) * HALO, HALO), :] = value[:, w * 128 : (w + 1) * 128]

    zeros8 = jnp.zeros((8, 128), F32)
    for row in range(2):
        shifted[row, pl.ds(0, 8), :] = zeros8
        shifted[row, pl.ds(8 + PAIRS, 8), :] = zeros8
    pair_ids = lax.broadcasted_iota(jnp.int32, (PAIRS, 128), 0)
    lane_low = lax.broadcasted_iota(jnp.int32, (PAIRS, 128), 1) < 64
    col_valid = pair_ids < valid_pairs
    low16 = lax.broadcasted_iota(jnp.int32, (16, 128), 1) < 64

    def spread(row, value, dst_ref, pair):
        shifted[row, pl.ds(8, PAIRS), :] = value
        after = shifted[row, pl.ds(9, PAIRS), :]
        before = shifted[row, pl.ds(7, PAIRS), :]
        dst_ref[pair, :, pl.ds(row * 256, 128)] = value.astype(BF)
        dst_ref[pair, :, pl.ds(row * 256 + 128, 128)] = jnp.where(lane_low, after, before).astype(BF)

    def stage_one(pair, carry):
        sides = []
        for row in range(2):
            parts = []
            for w in range(4):
                got = lifted[pl.ds(w * 16 * HALO + pair * 2 + row, 16, stride=HALO), :]
                turned = pltpu.roll(got, 64, 1)
                parts += [
                    jnp.where(low16, got, 0.0),
                    jnp.where(low16, 0.0, got),
                    jnp.where(low16, turned, 0.0),
                    jnp.where(low16, 0.0, turned),
                ]
            side = jnp.concatenate(parts, axis=0).astype(BF)
            sides.append(jnp.concatenate([side, side], axis=0))
        value = jnp.dot(uc[...], jnp.concatenate(sides, axis=1), preferred_element_type=F32)
        for row in range(2):
            global_row = first_row + pair * 2 + row
            keep = col_valid & ((global_row >= 0) & (global_row < valid_rows))
            rounded = jnp.where(keep, value[:, row * 128 : (row + 1) * 128], 0.0).astype(BF)
            fine[pair, :, pl.ds(row * 128, 128)] = rounded
            spread(row, silu(rounded.astype(F32)), act_in, pair)
        return carry

    lax.fori_loop(0, 14, stage_one, 0)

    def conv(src_ref, pair, w_ref):
        window = jnp.concatenate([src_ref[pair], src_ref[pair + 1]], axis=1)
        return jnp.dot(window, w_ref[...], preferred_element_type=F32)

    def stage_two(pair, carry):
        value = conv(act_in, pair, w1)
        for row in range(2):
            local_row = pair * 2 + row
            tile_row = lax.div(local_row + 7, 8)
            global_row = first_row + 1 + local_row
            gain = maps[tile_row, :, pl.ds(0, 128)]
            shift = maps[tile_row, :, pl.ds(128, 128)]
            keep = col_valid & ((global_row >= 0) & (global_row < valid_rows))
            moved = value[:, row * 128 : (row + 1) * 128] * gain + shift
            spread(row, jnp.where(keep, silu(moved), 0.0), hid_in, pair)
        return carry

    lax.fori_loop(0, 13, stage_two, 0)

    def stage_three(pair, carry):
        value = conv(hid_in, pair, w2)
        for row in range(2):
            global_row = first_row + 2 + pair * 2 + row
            keep = col_valid & (global_row < valid_rows)
            total = fine[pair + 1, :, pl.ds(row * 128, 128)].astype(F32) + value[:, row * 128 : (row + 1) * 128]
            at = pl.multiple_of((pair * 2 + row) * PAIRS, PAIRS)
            result[pl.ds(at, PAIRS), :] = jnp.where(keep, total, 0.0)
        return carry

    lax.fori_loop(0, 12, stage_three, 0)

    def emit(group, carry):
        for k in range(16):
            p = group * 16 + k
            got = [result[pl.ds(p + 8 * r * PAIRS, 8, stride=PAIRS), :] for r in range(3)]
            out_ref[:, pl.ds(pl.multiple_of(p * 128, 128), 128)] = jnp.concatenate(got, axis=0).astype(BF)
        return carry

    lax.fori_loop(0, PAIRS // 16, emit, 0)


def compute(scalars, *operands):
    vmem = pl.BlockSpec(memory_space=pltpu.VMEM)
    return pl.pallas_call(
        compute_kernel,
        out_shape=jax.ShapeDtypeStruct((ROWS, PAIRS * 128), BF),
        in_specs=[pl.BlockSpec(memory_space=pltpu.SMEM)] + [vmem] * len(operands),
        out_specs=vmem,
        scratch_shapes=[
            pltpu.VMEM((1024, 256), BF),
            pltpu.VMEM((1024, 256), BF),
            pltpu.VMEM((512, 512), BF),
            pltpu.VMEM((512, 128), F32),
            pltpu.VMEM((PAIRS, 512), BF),
            pltpu.VMEM((4 * 16 * HALO, 128), F32),
            pltpu.VMEM((14, PAIRS, 512), BF),
            pltpu.VMEM((13, PAIRS, 512), BF),
            pltpu.VMEM((14, PAIRS, 256), BF),
            pltpu.VMEM((5, PAIRS, 256), F32),
            pltpu.VMEM((2, PAIRS + 16, 128), F32),
            pltpu.VMEM((ROWS * PAIRS, 128), F32),
        ],
        compiler_params=pltpu.CompilerParams(vmem_limit_bytes=63 * 1024 * 1024),
        name="block",
    )(scalars, *operands)


def local(
    coarse,
    cover,
    sizes,
    tclass,
    up_rows,
    up_cols,
    lift,
    kernel_one,
    kernel_two,
    gain_table,
    shift_table,
):
    slab = lax.axis_index("slab")
    scalars = jnp.concatenate([cover[:, 0, 0, :].reshape(24), sizes.reshape(16)])
    up = exchange(scalars, coarse, up_rows)
    tile_rows = jnp.clip(3 * slab - 1 + jnp.arange(8, dtype=jnp.int32), 0, 47)
    classes = tclass[0][tile_rows]
    out = compute(scalars, up, lift, up_cols, kernel_one, kernel_two, classes, gain_table, shift_table)
    return out[None]


def solution(mesh):
    return jax.shard_map(
        local,
        mesh=mesh,
        in_specs=(
            P("region", "slab", None, None),
            P(),
            P(),
            P("region", None, None),
            P(),
            P(),
            P(),
            P(),
            P(),
            P(),
            P(),
        ),
        out_specs=P("region", "slab", None),
        check_vma=False,
    )
```

```python
import jax
import jax.numpy as jnp
from jax import lax
from jax.experimental import pallas as pl
from jax.experimental.pallas import tpu as pltpu
from jax.sharding import PartitionSpec as P

BF = jnp.bfloat16
F32 = jnp.float32
ROWS = 24
HALO = 32
PAIRS = 768
CHUNK = 128
BAND = 256
STRIDE = 776
EMIT = 96


def split_hi_lo(value):
    hi = value.astype(BF)
    lo = (value - hi.astype(F32)).astype(BF)
    return hi, lo


def silu(value):
    half = 0.5 * value
    return half + half * jnp.tanh(half)


def build_conv_weights(kernel_ref, out_ref):
    empty = jnp.zeros((64, 64), F32)
    for row_in in range(4):
        for slot, pixel in enumerate((0, 1, 2, -1)):
            for row_out in range(2):
                parts = []
                for pixel_out in range(2):
                    p = row_in - row_out
                    q = pixel - pixel_out + 1
                    if 0 <= p <= 2 and 0 <= q <= 2:
                        parts.append(kernel_ref[p, q].astype(F32))
                    else:
                        parts.append(empty)
                out_ref[pl.ds(row_in * 256 + slot * 64, 64), pl.ds(row_out * 128, 128)] = jnp.concatenate(
                    parts, axis=1
                ).astype(BF)


MESH = pl.DeviceIdType.MESH


def exchange_kernel(
    heads_ref,
    coarse_ref,
    up_ref,
    out_ref,
    cols_send,
    cols_recv,
    pick_send,
    pick_recv,
    rows_send,
    rows_recv,
    padded,
    weights,
    send_one,
    recv_one,
    send_two,
    recv_two,
    send_three,
    recv_three,
):
    region = lax.axis_index("region")
    slab = lax.axis_index("slab")

    barrier = pltpu.get_barrier_semaphore()

    def greet_slab(step, carry):
        pl.semaphore_signal(barrier, inc=1, device_id={"slab": lax.rem(slab + step, 16)}, device_id_type=MESH)
        return carry

    def greet_region(step, carry):
        pl.semaphore_signal(barrier, inc=1, device_id={"region": lax.rem(region + step, 8)}, device_id_type=MESH)
        return carry

    lax.fori_loop(1, 16, greet_slab, 0)
    lax.fori_loop(1, 8, greet_region, 0)
    for t in range(11):
        column = jnp.concatenate([coarse_ref[k, t] for k in range(4)], axis=0)
        cols_send[t] = column.astype(BF)
    pl.semaphore_wait(barrier, 22)

    def copy_one(t, source, target):
        return pltpu.make_async_remote_copy(
            src_ref=cols_send.at[t],
            dst_ref=cols_recv.at[source],
            send_sem=send_one.at[t],
            recv_sem=recv_one.at[source],
            device_id={"slab": target},
            device_id_type=MESH,
        )

    def start_one(t, carry):
        target = lax.rem(11 * slab + t, 16)

        @pl.when(target != slab)
        def _():
            copy_one(t, slab, target).start()

        @pl.when(target == slab)
        def _():
            cols_recv[slab] = cols_send[t]

        return carry

    lax.fori_loop(0, 11, start_one, 0)

    padded[pl.ds(0, 8), :] = jnp.zeros((8, 128), F32)
    padded[pl.ds(8, 384), :] = up_ref[...]
    padded[pl.ds(392, 8), :] = jnp.zeros((8, 128), F32)
    for s in range(16):
        hi, lo = split_hi_lo(padded[pl.ds(24 * s + 6, HALO), :])
        weights[pl.ds(s * HALO, HALO), pl.ds(0, 128)] = hi
        weights[pl.ds(s * HALO, HALO), pl.ds(128, 128)] = lo

    def wait_one(source, carry):
        t = lax.rem(slab + 5 * source, 16)

        @pl.when((t < 11) & (source != slab))
        def _():
            copy_one(0, source, slab).wait_recv()

        return carry

    lax.fori_loop(0, 16, wait_one, 0)

    def copy_two(target, source):
        return pltpu.make_async_remote_copy(
            src_ref=pick_send.at[target],
            dst_ref=pick_recv.at[source],
            send_sem=send_two.at[target],
            recv_sem=recv_two.at[source],
            device_id={"region": target},
            device_id_type=MESH,
        )

    for r in range(8):
        head = heads_ref[3 * r + 2]
        place = lax.rem(slab - head + 176, 16)
        wanted = lax.div(lax.rem(head + place, 176), 11)
        pick_send[r] = cols_recv[wanted]

        @pl.when(region != r)
        def _():
            copy_two(r, region).start()

    pick_recv[region] = pick_send[region]

    def wait_two(step, carry):
        copy_two(0, lax.rem(region + step, 8)).wait_recv()
        return carry

    lax.fori_loop(1, 8, wait_two, 0)

    first = heads_ref[3 * region] * 32 + heads_ref[3 * region + 1] * 8
    row = lax.broadcasted_iota(jnp.int32, (128, 256), 0)
    choose = (row + first == lax.broadcasted_iota(jnp.int32, (128, 256), 1)).astype(F32).astype(BF)
    gathered = jnp.concatenate([pick_recv[b] for b in range(8)], axis=0)
    patch = jnp.dot(choose, gathered, preferred_element_type=F32).astype(BF)
    patch = jnp.concatenate([patch, patch], axis=0)

    def copy_three(target, source):
        return pltpu.make_async_remote_copy(
            src_ref=rows_send.at[target],
            dst_ref=rows_recv.at[source],
            send_sem=send_three.at[target],
            recv_sem=recv_three.at[source],
            device_id={"slab": target},
            device_id_type=MESH,
        )

    for part in range(4):
        value = jnp.dot(weights[pl.ds(part * 128, 128), :], patch, preferred_element_type=F32)
        for k in range(4):
            s = part * 4 + k
            rows_send[s] = value[k * HALO : (k + 1) * HALO].astype(BF)

            @pl.when(slab != s)
            def _():
                copy_three(s, slab).start()

    rows_recv[slab] = rows_send[slab]

    def wait_three(step, carry):
        copy_three(0, lax.rem(slab + step, 16)).wait_recv()
        return carry

    lax.fori_loop(1, 16, wait_three, 0)
    out_ref[...] = rows_recv[...]

    def done_one(t, carry):
        @pl.when(lax.rem(11 * slab + t, 16) != slab)
        def _():
            copy_one(t, slab, slab).wait_send()

        return carry

    lax.fori_loop(0, 11, done_one, 0)

    def done_two(step, carry):
        copy_two(lax.rem(region + step, 8), region).wait_send()
        return carry

    lax.fori_loop(1, 8, done_two, 0)

    def done_three(step, carry):
        copy_three(lax.rem(slab + step, 16), slab).wait_send()
        return carry

    lax.fori_loop(1, 16, done_three, 0)


def exchange(heads, coarse, up_rows):
    vmem = pl.BlockSpec(memory_space=pltpu.VMEM)
    return pl.pallas_call(
        exchange_kernel,
        out_shape=jax.ShapeDtypeStruct((16, HALO, 256), BF),
        in_specs=[pl.BlockSpec(memory_space=pltpu.SMEM), vmem, vmem],
        out_specs=vmem,
        scratch_shapes=[
            pltpu.VMEM((11, 32, 256), BF),
            pltpu.VMEM((16, 32, 256), BF),
            pltpu.VMEM((8, 32, 256), BF),
            pltpu.VMEM((8, 32, 256), BF),
            pltpu.VMEM((16, HALO, 256), BF),
            pltpu.VMEM((16, HALO, 256), BF),
            pltpu.VMEM((400, 128), F32),
            pltpu.VMEM((512, 256), BF),
            pltpu.SemaphoreType.DMA((11,)),
            pltpu.SemaphoreType.DMA((16,)),
            pltpu.SemaphoreType.DMA((8,)),
            pltpu.SemaphoreType.DMA((8,)),
            pltpu.SemaphoreType.DMA((16,)),
            pltpu.SemaphoreType.DMA((16,)),
        ],
        compiler_params=pltpu.CompilerParams(collective_id=0, has_side_effects=True),
        name="exchange",
    )(heads, coarse, up_rows)


def prepare_columns(cols_ref, valid_pairs, split, uc):
    source = lax.broadcasted_iota(jnp.int32, (256, 256), 0)
    target = lax.broadcasted_iota(jnp.int32, (256, 256), 1)
    chosen = jnp.where(target < 128, 2 * target, 2 * target - 255)
    select = (source == chosen).astype(F32).astype(BF)
    pair = lax.broadcasted_iota(jnp.int32, (128, 256), 0)
    for chunk in range(6):
        halves = split_hi_lo(cols_ref[:, pl.ds(chunk * 256, 256)])
        for part in range(2):
            value = jnp.dot(halves[part], select, preferred_element_type=F32)
            split[pl.ds(part * 256, 128), :] = value[:, :128]
            split[pl.ds(part * 256 + 128, 128), :] = value[:, 128:]
        for part in range(2):
            pieces = []
            for w in range(4):
                for q, parity in ((0, 0), (1, 1), (1, 0), (0, 1)):
                    pieces.append(split[pl.ds(part * 256 + parity * 128 + 2 * w + q, 16, stride=8), :])
            block = jnp.concatenate(pieces, axis=0).T
            block = jnp.where(pair + chunk * 128 < valid_pairs, block, 0.0)
            uc[pl.ds(chunk * 128, 128), pl.ds(part * 256, 256)] = block.astype(BF)


def prepare_lift(lift_ref, lift_w):
    empty = jnp.zeros((32, 64), F32)
    lift_w[...] = jnp.zeros_like(lift_w)
    for part, value in enumerate(split_hi_lo(lift_ref[...])):
        value = value.astype(F32)
        sides = (jnp.concatenate([value, empty], axis=1), jnp.concatenate([empty, value], axis=1))
        for bw in range(8):
            lift_w[pl.ds(part * 256 + bw * 32, 32), pl.ds(bw // 2 * 128, 128)] = sides[bw % 2].astype(BF)


def prepare_maps(class_ref, gain_ref, shift_ref, size_rows, slab, valid_pairs, maps):
    gain, shift = gain_ref[...], shift_ref[...]
    table = jnp.concatenate(split_hi_lo(jnp.concatenate([gain, gain, shift, shift], axis=1)), axis=0)
    owner = lax.broadcasted_iota(jnp.int32, (192, PAIRS), 1) // 4
    inside = lax.broadcasted_iota(jnp.int32, (192, PAIRS), 1) < valid_pairs
    widen = (inside & (owner == lax.broadcasted_iota(jnp.int32, (192, PAIRS), 0))).astype(F32).astype(BF)
    ids = lax.broadcasted_iota(jnp.int32, (32, 192), 0) % 16
    hots = []
    for tile_row in range(5):
        place = 3 * slab - 1 + tile_row
        row_valid = (place >= 0) & (place < 3 * size_rows)
        hots.append((row_valid & (class_ref[pl.ds(tile_row, 1), :] == ids)).astype(F32))
    wide = jnp.dot(jnp.concatenate(hots, axis=0).astype(BF), widen, preferred_element_type=F32)
    for tile_row in range(5):
        hot = wide[tile_row * 32 : (tile_row + 1) * 32].T.astype(BF)
        maps[tile_row] = jnp.dot(hot, table, preferred_element_type=F32)


def compute_kernel(
    sc_ref,
    rows_ref,
    lift_ref,
    cols_ref,
    k1_ref,
    k2_ref,
    class_ref,
    gain_ref,
    shift_ref,
    out_ref,
    w1,
    w2,
    lift_w,
    split,
    uc,
    lifted,
    act_in,
    hid_in,
    fine,
    maps,
    act_out,
    hid_out,
    result,
    staged,
    sems,
):
    region = lax.axis_index("region")
    slab = lax.axis_index("slab")
    start = sc_ref[3 * region + 2]
    size_rows = sc_ref[24 + 2 * region]
    valid_pairs = sc_ref[25 + 2 * region] * 48

    build_conv_weights(k1_ref, w1)
    build_conv_weights(k2_ref, w2)
    prepare_columns(cols_ref, valid_pairs, split, uc)
    prepare_lift(lift_ref, lift_w)
    prepare_maps(class_ref, gain_ref, shift_ref, size_rows, slab, valid_pairs, maps)
    row = slab * 24 - 2 + lax.broadcasted_iota(jnp.int32, (HALO, 128), 0)
    row_valid = (row >= 0) & (row < size_rows * 24)
    for place in range(16):
        block = rows_ref[lax.rem(place + start, 16)]
        block = jnp.concatenate([block, block], axis=1)
        value = jnp.dot(block, lift_w[...], preferred_element_type=F32)
        for w in range(4):
            lifted[pl.ds((w * 16 + place) * HALO, HALO), :] = jnp.where(
                row_valid, value[:, w * 128 : (w + 1) * 128], 0.0
            )

    zeros8 = jnp.zeros((8, 128), F32)
    for buffer in (act_out, hid_out):
        for row in range(2):
            buffer[row, pl.ds(0, 8), :] = zeros8
            buffer[row, pl.ds(8 + PAIRS, 8), :] = zeros8
    low = lax.broadcasted_iota(jnp.int32, (CHUNK, 128), 1) < 64
    low16 = lax.broadcasted_iota(jnp.int32, (16, 128), 1) < 64

    def spread(src_ref, dst_ref, pair):
        for row in range(2):
            for c in range(0, PAIRS, CHUNK):
                own = src_ref[row, pl.ds(8 + c, CHUNK), :]
                after = src_ref[row, pl.ds(9 + c, CHUNK), :]
                before = src_ref[row, pl.ds(7 + c, CHUNK), :]
                dst_ref[pair, pl.ds(c, CHUNK), pl.ds(row * 256, 128)] = own.astype(BF)
                dst_ref[pair, pl.ds(c, CHUNK), pl.ds(row * 256 + 128, 128)] = jnp.where(low, after, before).astype(BF)

    def upsample(pair):
        sides = []
        for row in range(2):
            parts = []
            for w in range(4):
                got = lifted[pl.ds(w * 16 * HALO + pair * 2 + row, 16, stride=HALO), :]
                turned = pltpu.roll(got, 64, 1)
                parts += [
                    jnp.where(low16, got, 0.0),
                    jnp.where(low16, 0.0, got),
                    jnp.where(low16, turned, 0.0),
                    jnp.where(low16, 0.0, turned),
                ]
            side = jnp.concatenate(parts, axis=0).astype(BF)
            sides.append(jnp.concatenate([side, side], axis=0))
        side = jnp.concatenate(sides, axis=1)
        for c in range(0, PAIRS, BAND):
            value = jnp.dot(uc[pl.ds(c, BAND), :], side, preferred_element_type=F32)
            for row in range(2):
                rounded = value[:, row * 128 : (row + 1) * 128].astype(BF)
                fine[pair, pl.ds(c, BAND), pl.ds(row * 128, 128)] = rounded
                act_out[row, pl.ds(8 + c, BAND), :] = silu(rounded.astype(F32))

    def conv(src_ref, pair, c, w_ref):
        window = jnp.concatenate([src_ref[pair, pl.ds(c, BAND), :], src_ref[pair + 1, pl.ds(c, BAND), :]], axis=1)
        return jnp.dot(window, w_ref[...], preferred_element_type=F32)

    def first_conv(pair):
        for c in range(0, PAIRS, BAND):
            value = conv(act_in, pair, c, w1)
            for row in range(2):
                tile_row = lax.div(pair * 2 + row + 7, 8)
                gain = maps[tile_row, pl.ds(c, BAND), pl.ds(0, 128)]
                shift = maps[tile_row, pl.ds(c, BAND), pl.ds(128, 128)]
                hid_out[row, pl.ds(8 + c, BAND), :] = silu(value[:, row * 128 : (row + 1) * 128] * gain + shift)

    def second_conv(pair):
        for c in range(0, PAIRS, BAND):
            value = conv(hid_in, pair, c, w2)
            for row in range(2):
                total = fine[pair + 1, pl.ds(c, BAND), pl.ds(row * 128, 128)].astype(F32)
                at = pl.multiple_of((pair * 2 + row) * STRIDE + c, 8)
                result[pl.ds(at, BAND), :] = total + value[:, row * 128 : (row + 1) * 128]

    def steps(first, last, last_two=False, last_one=False, up=False, one=False, two=False):
        def body(k, carry):
            if two:
                second_conv(k - 6)
            if one or last_two:
                spread(hid_out, hid_in, jnp.clip(k - 4, 0, 12))
            if one:
                first_conv(k - 3)
            if up or last_one:
                spread(act_out, act_in, jnp.clip(k - 1, 0, 13))
            if up:
                upsample(k)
            return carry

        lax.fori_loop(first, last, body, 0)

    steps(0, 3, up=True)
    steps(3, 6, up=True, one=True)
    steps(6, 14, up=True, one=True, two=True)
    steps(14, 16, last_one=True, one=True, two=True)
    steps(16, 18, last_two=True, two=True)

    shown = jnp.where(slab < size_rows, valid_pairs, 0)

    def copy_out(chunk):
        span = pl.ds(pl.multiple_of(chunk * (EMIT * 128), EMIT * 128), EMIT * 128)
        return pltpu.make_async_copy(staged.at[:, span], out_ref.at[:, span], sems.at[chunk])

    def emit(chunk, carry):
        def inner(group, carry):
            for k in range(16):
                p = chunk * EMIT + group * 16 + k
                got = [result[pl.ds(p + 8 * r * STRIDE, 8, stride=STRIDE), :] for r in range(3)]
                value = jnp.where(p < shown, jnp.concatenate(got, axis=0), 0.0)
                staged[:, pl.ds(pl.multiple_of(p * 128, 128), 128)] = value.astype(BF)
            return carry

        lax.fori_loop(0, EMIT // 16, inner, 0)
        copy_out(chunk).start()
        return carry

    lax.fori_loop(0, PAIRS // EMIT, emit, 0)

    def drain(chunk, carry):
        copy_out(chunk).wait()
        return carry

    lax.fori_loop(0, PAIRS // EMIT, drain, 0)


def compute(scalars, *operands):
    vmem = pl.BlockSpec(memory_space=pltpu.VMEM)
    return pl.pallas_call(
        compute_kernel,
        out_shape=jax.ShapeDtypeStruct((ROWS, PAIRS * 128), BF),
        in_specs=[pl.BlockSpec(memory_space=pltpu.SMEM)] + [vmem] * len(operands),
        out_specs=pl.BlockSpec(memory_space=pltpu.HBM),
        scratch_shapes=[
            pltpu.VMEM((1024, 256), BF),
            pltpu.VMEM((1024, 256), BF),
            pltpu.VMEM((512, 512), BF),
            pltpu.VMEM((512, 128), F32),
            pltpu.VMEM((PAIRS, 512), BF),
            pltpu.VMEM((4 * 16 * HALO, 128), F32),
            pltpu.VMEM((14, PAIRS, 512), BF),
            pltpu.VMEM((13, PAIRS, 512), BF),
            pltpu.VMEM((14, PAIRS, 256), BF),
            pltpu.VMEM((5, PAIRS, 256), F32),
            pltpu.VMEM((2, PAIRS + 16, 128), F32),
            pltpu.VMEM((2, PAIRS + 16, 128), F32),
            pltpu.VMEM((ROWS * STRIDE, 128), F32),
            pltpu.VMEM((ROWS, PAIRS * 128), BF),
            pltpu.SemaphoreType.DMA((PAIRS // EMIT,)),
        ],
        compiler_params=pltpu.CompilerParams(vmem_limit_bytes=63 * 1024 * 1024),
        name="block",
    )(scalars, *operands)


def local(
    coarse,
    cover,
    sizes,
    tclass,
    up_rows,
    up_cols,
    lift,
    kernel_one,
    kernel_two,
    gain_table,
    shift_table,
):
    slab = lax.axis_index("slab")
    scalars = jnp.concatenate([cover[:, 0, 0, :].reshape(24), sizes.reshape(16)])
    up = exchange(scalars, coarse, up_rows)
    tile_rows = jnp.clip(3 * slab - 1 + jnp.arange(8, dtype=jnp.int32), 0, 47)
    classes = tclass[0][tile_rows]
    out = compute(scalars, up, lift, up_cols, kernel_one, kernel_two, classes, gain_table, shift_table)
    return out[None]


def solution(mesh):
    return jax.shard_map(
        local,
        mesh=mesh,
        in_specs=(
            P("region", "slab", None, None),
            P(),
            P(),
            P("region", None, None),
            P(),
            P(),
            P(),
            P(),
            P(),
            P(),
            P(),
        ),
        out_specs=P("region", "slab", None),
        check_vma=False,
    )
```

```python
import jax
import jax.numpy as jnp
from jax import lax
from jax.experimental import pallas as pl
from jax.experimental.pallas import tpu as pltpu
from jax.sharding import PartitionSpec as P

BF = jnp.bfloat16
F32 = jnp.float32
ROWS = 24
HALO = 32
PAIRS = 768
CHUNK = 128
BAND = 256
STRIDE = 776
EMIT = 96


def split_hi_lo(value):
    hi = value.astype(BF)
    lo = (value - hi.astype(F32)).astype(BF)
    return hi, lo


def silu(value):
    half = 0.5 * value
    return half + half * jnp.tanh(half)


def build_conv_weights(kernel_ref, out_ref):
    empty = jnp.zeros((64, 64), F32)
    for row_in in range(4):
        for slot, pixel in enumerate((0, 1, 2, -1)):
            for row_out in range(2):
                parts = []
                for pixel_out in range(2):
                    p = row_in - row_out
                    q = pixel - pixel_out + 1
                    if 0 <= p <= 2 and 0 <= q <= 2:
                        parts.append(kernel_ref[p, q].astype(F32))
                    else:
                        parts.append(empty)
                out_ref[pl.ds(row_in * 256 + slot * 64, 64), pl.ds(row_out * 128, 128)] = jnp.concatenate(
                    parts, axis=1
                ).astype(BF)


MESH = pl.DeviceIdType.MESH


def exchange_kernel(
    cover_ref,
    coarse_ref,
    up_ref,
    out_ref,
    cols_send,
    cols_recv,
    pick_send,
    pick_recv,
    rows_send,
    rows_recv,
    padded,
    weights,
    heads,
    heads_sem,
    send_one,
    recv_one,
    send_two,
    recv_two,
    send_three,
    recv_three,
):
    region = lax.axis_index("region")
    slab = lax.axis_index("slab")

    fetch = pltpu.make_async_copy(cover_ref.at[:, :, 0, :], heads, heads_sem)
    fetch.start()
    barrier = pltpu.get_barrier_semaphore()

    def greet_slab(step, carry):
        pl.semaphore_signal(barrier, inc=1, device_id={"slab": lax.rem(slab + step, 16)}, device_id_type=MESH)
        return carry

    def greet_region(step, carry):
        pl.semaphore_signal(barrier, inc=1, device_id={"region": lax.rem(region + step, 8)}, device_id_type=MESH)
        return carry

    lax.fori_loop(1, 16, greet_slab, 0)
    lax.fori_loop(1, 8, greet_region, 0)
    for t in range(11):
        column = jnp.concatenate([coarse_ref[k, t] for k in range(4)], axis=0)
        cols_send[t] = column.astype(BF)
    pl.semaphore_wait(barrier, 22)

    def copy_one(t, source, target):
        return pltpu.make_async_remote_copy(
            src_ref=cols_send.at[t],
            dst_ref=cols_recv.at[source],
            send_sem=send_one.at[t],
            recv_sem=recv_one.at[source],
            device_id={"slab": target},
            device_id_type=MESH,
        )

    def start_one(t, carry):
        target = lax.rem(11 * slab + t, 16)

        @pl.when(target != slab)
        def _():
            copy_one(t, slab, target).start()

        @pl.when(target == slab)
        def _():
            cols_recv[slab] = cols_send[t]

        return carry

    lax.fori_loop(0, 11, start_one, 0)

    padded[pl.ds(0, 8), :] = jnp.zeros((8, 128), F32)
    padded[pl.ds(8, 384), :] = up_ref[...]
    padded[pl.ds(392, 8), :] = jnp.zeros((8, 128), F32)
    for s in range(16):
        hi, lo = split_hi_lo(padded[pl.ds(24 * s + 6, HALO), :])
        weights[pl.ds(s * HALO, HALO), pl.ds(0, 128)] = hi
        weights[pl.ds(s * HALO, HALO), pl.ds(128, 128)] = lo

    def wait_one(source, carry):
        t = lax.rem(slab + 5 * source, 16)

        @pl.when((t < 11) & (source != slab))
        def _():
            copy_one(0, source, slab).wait_recv()

        return carry

    lax.fori_loop(0, 16, wait_one, 0)

    def copy_two(target, source):
        return pltpu.make_async_remote_copy(
            src_ref=pick_send.at[target],
            dst_ref=pick_recv.at[source],
            send_sem=send_two.at[target],
            recv_sem=recv_two.at[source],
            device_id={"region": target},
            device_id_type=MESH,
        )

    fetch.wait()
    for r in range(8):
        head = heads[r, 2, 0]
        place = lax.rem(slab - head + 176, 16)
        wanted = lax.div(lax.rem(head + place, 176), 11)
        pick_send[r] = cols_recv[wanted]

        @pl.when(region != r)
        def _():
            copy_two(r, region).start()

    pick_recv[region] = pick_send[region]

    def wait_two(step, carry):
        copy_two(0, lax.rem(region + step, 8)).wait_recv()
        return carry

    lax.fori_loop(1, 8, wait_two, 0)

    first = heads[region, 0, 0] * 32 + heads[region, 1, 0] * 8
    row = lax.broadcasted_iota(jnp.int32, (128, 256), 0)
    choose = (row + first == lax.broadcasted_iota(jnp.int32, (128, 256), 1)).astype(F32).astype(BF)
    gathered = jnp.concatenate([pick_recv[b] for b in range(8)], axis=0)
    patch = jnp.dot(choose, gathered, preferred_element_type=F32).astype(BF)
    patch = jnp.concatenate([patch, patch], axis=0)

    def copy_three(target, source):
        return pltpu.make_async_remote_copy(
            src_ref=rows_send.at[target],
            dst_ref=rows_recv.at[source],
            send_sem=send_three.at[target],
            recv_sem=recv_three.at[source],
            device_id={"slab": target},
            device_id_type=MESH,
        )

    for part in range(4):
        value = jnp.dot(weights[pl.ds(part * 128, 128), :], patch, preferred_element_type=F32)
        for k in range(4):
            s = part * 4 + k
            rows_send[s] = value[k * HALO : (k + 1) * HALO].astype(BF)

            @pl.when(slab != s)
            def _():
                copy_three(s, slab).start()

    rows_recv[slab] = rows_send[slab]

    def wait_three(step, carry):
        copy_three(0, lax.rem(slab + step, 16)).wait_recv()
        return carry

    lax.fori_loop(1, 16, wait_three, 0)
    start = heads[region, 2, 0]
    for place in range(16):
        out_ref[place] = rows_recv[lax.rem(place + start, 16)]

    def done_one(t, carry):
        @pl.when(lax.rem(11 * slab + t, 16) != slab)
        def _():
            copy_one(t, slab, slab).wait_send()

        return carry

    lax.fori_loop(0, 11, done_one, 0)

    def done_two(step, carry):
        copy_two(lax.rem(region + step, 8), region).wait_send()
        return carry

    lax.fori_loop(1, 8, done_two, 0)

    def done_three(step, carry):
        copy_three(lax.rem(slab + step, 16), slab).wait_send()
        return carry

    lax.fori_loop(1, 16, done_three, 0)


def exchange(cover, coarse, up_rows):
    vmem = pl.BlockSpec(memory_space=pltpu.VMEM)
    return pl.pallas_call(
        exchange_kernel,
        out_shape=jax.ShapeDtypeStruct((16, HALO, 256), BF),
        in_specs=[pl.BlockSpec(memory_space=pltpu.HBM), vmem, vmem],
        out_specs=vmem,
        scratch_shapes=[
            pltpu.VMEM((11, 32, 256), BF),
            pltpu.VMEM((16, 32, 256), BF),
            pltpu.VMEM((8, 32, 256), BF),
            pltpu.VMEM((8, 32, 256), BF),
            pltpu.VMEM((16, HALO, 256), BF),
            pltpu.VMEM((16, HALO, 256), BF),
            pltpu.VMEM((400, 128), F32),
            pltpu.VMEM((512, 256), BF),
            pltpu.SMEM((8, 3, 16), jnp.int32),
            pltpu.SemaphoreType.DMA,
            pltpu.SemaphoreType.DMA((11,)),
            pltpu.SemaphoreType.DMA((16,)),
            pltpu.SemaphoreType.DMA((8,)),
            pltpu.SemaphoreType.DMA((8,)),
            pltpu.SemaphoreType.DMA((16,)),
            pltpu.SemaphoreType.DMA((16,)),
        ],
        compiler_params=pltpu.CompilerParams(collective_id=0, has_side_effects=True),
        name="exchange",
    )(cover, coarse, up_rows)


def prepare_columns(cols_ref, valid_pairs, split, uc):
    source = lax.broadcasted_iota(jnp.int32, (256, 256), 0)
    target = lax.broadcasted_iota(jnp.int32, (256, 256), 1)
    chosen = jnp.where(target < 128, 2 * target, 2 * target - 255)
    select = (source == chosen).astype(F32).astype(BF)
    pair = lax.broadcasted_iota(jnp.int32, (128, 256), 0)
    for chunk in range(6):
        halves = split_hi_lo(cols_ref[:, pl.ds(chunk * 256, 256)])
        for part in range(2):
            value = jnp.dot(halves[part], select, preferred_element_type=F32)
            split[pl.ds(part * 256, 128), :] = value[:, :128]
            split[pl.ds(part * 256 + 128, 128), :] = value[:, 128:]
        for part in range(2):
            pieces = []
            for w in range(4):
                for q, parity in ((0, 0), (1, 1), (1, 0), (0, 1)):
                    pieces.append(split[pl.ds(part * 256 + parity * 128 + 2 * w + q, 16, stride=8), :])
            block = jnp.concatenate(pieces, axis=0).T
            block = jnp.where(pair + chunk * 128 < valid_pairs, block, 0.0)
            uc[pl.ds(chunk * 128, 128), pl.ds(part * 256, 256)] = block.astype(BF)


def prepare_lift(lift_ref, lift_w):
    empty = jnp.zeros((32, 64), F32)
    lift_w[...] = jnp.zeros_like(lift_w)
    for part, value in enumerate(split_hi_lo(lift_ref[...])):
        value = value.astype(F32)
        sides = (jnp.concatenate([value, empty], axis=1), jnp.concatenate([empty, value], axis=1))
        for bw in range(8):
            lift_w[pl.ds(part * 256 + bw * 32, 32), pl.ds(bw // 2 * 128, 128)] = sides[bw % 2].astype(BF)


def prepare_maps(class_ref, gain_ref, shift_ref, size_rows, slab, valid_pairs, maps):
    gain, shift = gain_ref[...], shift_ref[...]
    table = jnp.concatenate(split_hi_lo(jnp.concatenate([gain, gain, shift, shift], axis=1)), axis=0)
    owner = lax.broadcasted_iota(jnp.int32, (192, PAIRS), 1) // 4
    inside = lax.broadcasted_iota(jnp.int32, (192, PAIRS), 1) < valid_pairs
    widen = (inside & (owner == lax.broadcasted_iota(jnp.int32, (192, PAIRS), 0))).astype(F32).astype(BF)
    ids = lax.broadcasted_iota(jnp.int32, (32, 192), 0) % 16
    hots = []
    for tile_row in range(5):
        place = 3 * slab - 1 + tile_row
        row_valid = (place >= 0) & (place < 3 * size_rows)
        classes = class_ref[pl.ds(jnp.clip(place, 0, 47), 1), :]
        hots.append((row_valid & (classes == ids)).astype(F32))
    wide = jnp.dot(jnp.concatenate(hots, axis=0).astype(BF), widen, preferred_element_type=F32)
    for tile_row in range(5):
        hot = wide[tile_row * 32 : (tile_row + 1) * 32].T.astype(BF)
        maps[tile_row] = jnp.dot(hot, table, preferred_element_type=F32)


def compute_kernel(
    sc_ref,
    rows_ref,
    lift_ref,
    cols_ref,
    k1_ref,
    k2_ref,
    class_ref,
    gain_ref,
    shift_ref,
    out_ref,
    w1,
    w2,
    lift_w,
    split,
    uc,
    lifted,
    act_in,
    hid_in,
    fine,
    maps,
    act_out,
    hid_out,
    result,
    staged,
    sems,
):
    region = lax.axis_index("region")
    slab = lax.axis_index("slab")
    size_rows = sc_ref[0, region]
    valid_pairs = sc_ref[1, region] * 48

    build_conv_weights(k1_ref, w1)
    build_conv_weights(k2_ref, w2)
    prepare_columns(cols_ref, valid_pairs, split, uc)
    prepare_lift(lift_ref, lift_w)
    prepare_maps(class_ref, gain_ref, shift_ref, size_rows, slab, valid_pairs, maps)
    row = slab * 24 - 2 + lax.broadcasted_iota(jnp.int32, (HALO, 128), 0)
    row_valid = (row >= 0) & (row < size_rows * 24)
    for place in range(16):
        block = rows_ref[place]
        block = jnp.concatenate([block, block], axis=1)
        value = jnp.dot(block, lift_w[...], preferred_element_type=F32)
        for w in range(4):
            lifted[pl.ds((w * 16 + place) * HALO, HALO), :] = jnp.where(
                row_valid, value[:, w * 128 : (w + 1) * 128], 0.0
            )

    zeros8 = jnp.zeros((8, 128), F32)
    for buffer in (act_out, hid_out):
        for row in range(2):
            buffer[row, pl.ds(0, 8), :] = zeros8
            buffer[row, pl.ds(8 + PAIRS, 8), :] = zeros8
    low = lax.broadcasted_iota(jnp.int32, (CHUNK, 128), 1) < 64
    low16 = lax.broadcasted_iota(jnp.int32, (16, 128), 1) < 64

    def spread(src_ref, dst_ref, pair):
        for row in range(2):
            for c in range(0, PAIRS, CHUNK):
                own = src_ref[row, pl.ds(8 + c, CHUNK), :]
                after = src_ref[row, pl.ds(9 + c, CHUNK), :]
                before = src_ref[row, pl.ds(7 + c, CHUNK), :]
                dst_ref[pair, pl.ds(c, CHUNK), pl.ds(row * 256, 128)] = own.astype(BF)
                dst_ref[pair, pl.ds(c, CHUNK), pl.ds(row * 256 + 128, 128)] = jnp.where(low, after, before).astype(BF)

    def upsample(pair):
        sides = []
        for row in range(2):
            parts = []
            for w in range(4):
                got = lifted[pl.ds(w * 16 * HALO + pair * 2 + row, 16, stride=HALO), :]
                turned = pltpu.roll(got, 64, 1)
                parts += [
                    jnp.where(low16, got, 0.0),
                    jnp.where(low16, 0.0, got),
                    jnp.where(low16, turned, 0.0),
                    jnp.where(low16, 0.0, turned),
                ]
            side = jnp.concatenate(parts, axis=0).astype(BF)
            sides.append(jnp.concatenate([side, side], axis=0))
        side = jnp.concatenate(sides, axis=1)
        for c in range(0, PAIRS, BAND):
            value = jnp.dot(uc[pl.ds(c, BAND), :], side, preferred_element_type=F32)
            for row in range(2):
                rounded = value[:, row * 128 : (row + 1) * 128].astype(BF)
                fine[pair, pl.ds(c, BAND), pl.ds(row * 128, 128)] = rounded
                act_out[row, pl.ds(8 + c, BAND), :] = silu(rounded.astype(F32))

    def conv(src_ref, pair, c, w_ref):
        window = jnp.concatenate([src_ref[pair, pl.ds(c, BAND), :], src_ref[pair + 1, pl.ds(c, BAND), :]], axis=1)
        return jnp.dot(window, w_ref[...], preferred_element_type=F32)

    def first_conv(pair):
        for c in range(0, PAIRS, BAND):
            value = conv(act_in, pair, c, w1)
            for row in range(2):
                tile_row = lax.div(pair * 2 + row + 7, 8)
                gain = maps[tile_row, pl.ds(c, BAND), pl.ds(0, 128)]
                shift = maps[tile_row, pl.ds(c, BAND), pl.ds(128, 128)]
                hid_out[row, pl.ds(8 + c, BAND), :] = silu(value[:, row * 128 : (row + 1) * 128] * gain + shift)

    def second_conv(pair):
        for c in range(0, PAIRS, BAND):
            value = conv(hid_in, pair, c, w2)
            for row in range(2):
                total = fine[pair + 1, pl.ds(c, BAND), pl.ds(row * 128, 128)].astype(F32)
                at = pl.multiple_of((pair * 2 + row) * STRIDE + c, 8)
                result[pl.ds(at, BAND), :] = total + value[:, row * 128 : (row + 1) * 128]

    def steps(first, last, last_two=False, last_one=False, up=False, one=False, two=False):
        def body(k, carry):
            if two:
                second_conv(k - 6)
            if one or last_two:
                spread(hid_out, hid_in, jnp.clip(k - 4, 0, 12))
            if one:
                first_conv(k - 3)
            if up or last_one:
                spread(act_out, act_in, jnp.clip(k - 1, 0, 13))
            if up:
                upsample(k)
            return carry

        lax.fori_loop(first, last, body, 0)

    steps(0, 3, up=True)
    steps(3, 6, up=True, one=True)
    steps(6, 14, up=True, one=True, two=True)
    steps(14, 16, last_one=True, one=True, two=True)
    steps(16, 18, last_two=True, two=True)

    shown = jnp.where(slab < size_rows, valid_pairs, 0)

    def copy_out(chunk):
        span = pl.ds(pl.multiple_of(chunk * (EMIT * 128), EMIT * 128), EMIT * 128)
        return pltpu.make_async_copy(staged.at[:, span], out_ref.at[:, span], sems.at[chunk])

    def emit(chunk, carry):
        def inner(group, carry):
            for k in range(16):
                p = chunk * EMIT + group * 16 + k
                got = [result[pl.ds(p + 8 * r * STRIDE, 8, stride=STRIDE), :] for r in range(3)]
                value = jnp.where(p < shown, jnp.concatenate(got, axis=0), 0.0)
                staged[:, pl.ds(pl.multiple_of(p * 128, 128), 128)] = value.astype(BF)
            return carry

        lax.fori_loop(0, EMIT // 16, inner, 0)
        copy_out(chunk).start()
        return carry

    lax.fori_loop(0, PAIRS // EMIT, emit, 0)

    def drain(chunk, carry):
        copy_out(chunk).wait()
        return carry

    lax.fori_loop(0, PAIRS // EMIT, drain, 0)


def compute(scalars, *operands):
    vmem = pl.BlockSpec(memory_space=pltpu.VMEM)
    return pl.pallas_call(
        compute_kernel,
        out_shape=jax.ShapeDtypeStruct((ROWS, PAIRS * 128), BF),
        in_specs=[pl.BlockSpec(memory_space=pltpu.SMEM)] + [vmem] * len(operands),
        out_specs=pl.BlockSpec(memory_space=pltpu.HBM),
        scratch_shapes=[
            pltpu.VMEM((1024, 256), BF),
            pltpu.VMEM((1024, 256), BF),
            pltpu.VMEM((512, 512), BF),
            pltpu.VMEM((512, 128), F32),
            pltpu.VMEM((PAIRS, 512), BF),
            pltpu.VMEM((4 * 16 * HALO, 128), F32),
            pltpu.VMEM((14, PAIRS, 512), BF),
            pltpu.VMEM((13, PAIRS, 512), BF),
            pltpu.VMEM((14, PAIRS, 256), BF),
            pltpu.VMEM((5, PAIRS, 256), F32),
            pltpu.VMEM((2, PAIRS + 16, 128), F32),
            pltpu.VMEM((2, PAIRS + 16, 128), F32),
            pltpu.VMEM((ROWS * STRIDE, 128), F32),
            pltpu.VMEM((ROWS, PAIRS * 128), BF),
            pltpu.SemaphoreType.DMA((PAIRS // EMIT,)),
        ],
        compiler_params=pltpu.CompilerParams(vmem_limit_bytes=63 * 1024 * 1024),
        name="block",
    )(scalars, *operands)


def local(
    coarse,
    cover,
    sizes,
    tclass,
    up_rows,
    up_cols,
    lift,
    kernel_one,
    kernel_two,
    gain_table,
    shift_table,
):
    up = exchange(jnp.transpose(cover, (0, 3, 1, 2)), coarse, up_rows)
    out = compute(sizes.T, up, lift, up_cols, kernel_one, kernel_two, tclass[0], gain_table, shift_table)
    return out[None]


def solution(mesh):
    return jax.shard_map(
        local,
        mesh=mesh,
        in_specs=(
            P("region", "slab", None, None),
            P(),
            P(),
            P("region", None, None),
            P(),
            P(),
            P(),
            P(),
            P(),
            P(),
            P(),
        ),
        out_specs=P("region", "slab", None),
        check_vma=False,
    )
```
